32 devices in a mesh: sub: 4 (over x, core), slab: 8 (over z, y).
Axes of the slice: x: 2, y: 2, z: 4, core: 2. Of those that a mesh axis runs over, the one named last changes fastest.
Arguments:
- source: float32 [4, 256, 256, 256], P('sub', 'slab'), may hold values from -6 to 6
- coarse: float32 [2, 4, 256, 256, 256], P(None, 'sub', 'slab'), may hold values from -4 to 4
- rho: float32 [4], replicated, may hold values from 0.3 to 45, as said below
- basis_x: float32 [256, 256], replicated, may hold values from -0.375 to 0.375
- basis_y: float32 [256, 256], replicated, may hold values from -0.375 to 0.375
- basis_z: float32 [256, 256], replicated, may hold values from -0.375 to 0.375
- eigen_x: float32 [256], replicated, may hold values from 0.1 to 3
- eigen_y: float32 [256], replicated, may hold values from 0.1 to 3
- eigen_z: float32 [256], replicated, may hold values from 0.1 to 3
- face_stiff: float32 [256, 256], replicated, may hold values from 0.2 to 2
Outputs:
- solution: float32 [4, 256, 256, 256], P('sub', 'slab')
- multipliers: float32 [4, 256, 256], P('sub', 'slab')
- jump: float32 [4, 256, 256], P('sub', 'slab')
The draws below stay inside these ranges and needn't reach their ends.
Inputs may be any that keep to these rules, and one draw needn't show every extreme that they name: `rho`: positive coefficient of each subdomain.
All inputs are finite; a program needn't handle non-finite values.
Results may differ from the reference program's by a relative error of at most 0.00014.
Values sent between devices are 32-bit elements; how exact they have to be, the bound alone decides.
A program may use at most 128 MiB of HBM per device.

```python
import math
import jax
import jax.numpy as jnp
from jax import lax

N = 256
ITERS = 2
SUBS = 4


def draw_rho(key, part):
    place = jnp.arange(SUBS, dtype=jnp.float32) / max(SUBS - 1, 1)
    jitter = jax.random.uniform(key, (SUBS,), jnp.float32, 0.7, 1.4)
    return jnp.exp(jnp.log(10.0) * place) * jitter


def steps_of(rng, shape, shards, low, top_value):
    factor_of, own = 1.0, jax.random.fold_in(rng, 6)
    for axis_at, shards_of in shards:
        draws = jnp.exp(jax.random.uniform(jax.random.fold_in(own, axis_at), (shards_of,), jnp.float32, low / len(shards), top_value / len(shards)))
        factor_of = factor_of * jnp.repeat(draws, shape[axis_at] // shards_of).reshape([-1 if axis == axis_at else 1 for axis in range(len(shape))])
    return factor_of


def scatter_about(stream_key, shape, scale, reach, split=(), kind=jnp.bfloat16):
    gain = steps_of(stream_key, shape, split, -0.22, 0.18) if split else 1.0
    result = jax.random.normal(stream_key, shape, jnp.float32) * scale * gain
    return jnp.minimum(jnp.maximum(result, -reach), reach).astype(kind)


def setup_inputs(seed: int = 0) -> dict:
    seeds = jax.random.split(jax.random.key(seed), 11)
    return {
        "source": scatter_about(seeds[0], (SUBS, N, N, N), 1.0, 6.0, ((0, 4), (1, 8)), jnp.float32),
        "coarse": scatter_about(seeds[1], (ITERS, SUBS, N, N, N), 0.5, 4.0, ((1, 4), (2, 8)), jnp.float32),
        "rho": draw_rho(jax.random.fold_in(seeds[10], 71), 0),
        "basis_x": scatter_about(seeds[3], (N, N), N ** -0.5, 0.375, (), jnp.float32),
        "basis_y": scatter_about(seeds[4], (N, N), N ** -0.5, 0.375, (), jnp.float32),
        "basis_z": scatter_about(seeds[5], (N, N), N ** -0.5, 0.375, (), jnp.float32),
        "eigen_x": jnp.clip(jnp.exp(jax.random.uniform(seeds[6], (N,), jnp.float32, math.log(0.1), math.log(3.0))), 0.1, 3.0),
        "eigen_y": jnp.clip(jnp.exp(jax.random.uniform(seeds[7], (N,), jnp.float32, math.log(0.1), math.log(3.0))), 0.1, 3.0),
        "eigen_z": jnp.clip(jnp.exp(jax.random.uniform(seeds[8], (N,), jnp.float32, math.log(0.1), math.log(3.0))), 0.1, 3.0),
        "face_stiff": jnp.clip(jnp.exp(jax.random.uniform(seeds[9], (N, N), jnp.float32, math.log(0.2), math.log(2.0))), 0.2, 2.0),
    }


HI = lax.Precision.HIGHEST


def forward(field, basis_x, basis_y, basis_z):
    part = jnp.einsum('xyz,zk->xyk', field, basis_z, precision=HI)
    part = jnp.einsum('xyk,yj->xjk', part, basis_y, precision=HI)
    return jnp.einsum('xjk,xi->ijk', part, basis_x, precision=HI)


def inverse(modes, basis_x, basis_y, basis_z):
    part = jnp.einsum('ijk,xi->xjk', modes, basis_x, precision=HI)
    part = jnp.einsum('xjk,yj->xyk', part, basis_y, precision=HI)
    return jnp.einsum('xyk,zk->xyz', part, basis_z, precision=HI)


def reference(source, coarse, rho, basis_x, basis_y, basis_z, eigen_x, eigen_y, eigen_z, face_stiff):
    denom = eigen_x[:, None, None] + eigen_y[None, :, None] + eigen_z[None, None, :]

    def solve_one(pair):
        field, coeff = pair
        modes = forward(field, basis_x, basis_y, basis_z) / (denom * coeff)
        return inverse(modes, basis_x, basis_y, basis_z)

    weights = 0.5 * (rho + jnp.roll(rho, -1))
    multipliers = jnp.zeros((SUBS, N, N), jnp.float32)
    solution = source
    jump = multipliers
    for step in range(ITERS):
        earlier = jnp.roll(multipliers, 1, axis=0)
        load = source + coarse[step]
        load = load.at[:, :, :, N - 1].add(-multipliers)
        load = load.at[:, :, :, 0].add(earlier)
        solution = lax.map(solve_one, (load, rho))
        jump = solution[:, :, :, N - 1] - jnp.roll(solution[:, :, :, 0], -1, axis=0)
        face = jnp.einsum('sxy,yj->sxj', jump, basis_y, precision=HI)
        face = jnp.einsum('sxj,xi->sij', face, basis_x, precision=HI)
        face = face * face_stiff[None]
        face = jnp.einsum('sij,xi->sxj', face, basis_x, precision=HI)
        face = jnp.einsum('sxj,yj->sxy', face, basis_y, precision=HI)
        search = weights[:, None, None] * face
        alpha = jnp.sum(jump * search) / (jnp.sum(search * search) + 1e-6)
        multipliers = multipliers + alpha * search
    return solution, multipliers, jump
```

```python
import functools

import jax
import jax.numpy as jnp
from jax import lax
from jax.experimental import pallas as pl
from jax.experimental.pallas import tpu as pltpu
from jax.sharding import PartitionSpec as P

ITERS = 2
CHUNKS = 4

HI = lax.Precision.HIGHEST
MID = lax.Precision.HIGH
F32 = jnp.float32
BF16 = jnp.bfloat16


def split(value):
    top = value.astype(BF16)
    return top, (value - top.astype(F32)).astype(BF16)


def edge_kernel(part_ref, basis_ref, pair_ref, eigen_ref, first_ref, last_ref, out_ref):
    top, low = split(basis_ref[...])
    right = jnp.concatenate([top, low, top], axis=0)
    for at in range(part_ref.shape[0]):
        top, low = split(part_ref[at])
        left = jnp.concatenate([top, top, low], axis=0)
        hat = lax.dot_general(left, right, (((0,), (0,)), ((), ())), preferred_element_type=F32)
        modes = hat / (pair_ref[at : at + 1, :] + eigen_ref[...])
        out_ref[at, 0:1, :] = jnp.sum(modes * first_ref[...], axis=0, keepdims=True)
        out_ref[at, 1:2, :] = jnp.sum(modes * last_ref[...], axis=0, keepdims=True)


def partial_edges(part, basis_rows, pair, eigen, first, last):
    width, rows, depth = part.shape
    block = 8
    whole = lambda j: (0, 0)
    return pl.pallas_call(
        edge_kernel,
        out_shape=jax.ShapeDtypeStruct((width, 2, width), F32),
        grid=(width // block,),
        in_specs=[
            pl.BlockSpec((block, rows, depth), lambda j: (j, 0, 0)),
            pl.BlockSpec((rows, width), whole),
            pl.BlockSpec((block, width), lambda j: (j, 0)),
            pl.BlockSpec((depth, width), whole),
            pl.BlockSpec((depth, width), whole),
            pl.BlockSpec((depth, width), whole),
        ],
        out_specs=pl.BlockSpec((block, 2, width), lambda j: (j, 0, 0)),
        compiler_params=pltpu.CompilerParams(vmem_limit_bytes=24 * 2**20),
        cost_estimate=pl.CostEstimate(
            flops=2 * width * width * depth * 96, bytes_accessed=4 * width * rows * depth, transcendentals=0
        ),
        name="partial_edges",
    )(part, basis_rows, pair, eigen, first, last)


def face_step(edges, rho, basis_x, basis_y, face_stiff):
    apart = edges[:, :, 1] - jnp.roll(edges[:, :, 0], -1, axis=0)
    jump = jnp.einsum("sji,yj->syi", apart, basis_y, precision=HI)
    jump = jnp.einsum("syi,xi->sxy", jump, basis_x, precision=HI)
    face = jnp.einsum("sxy,yj->sxj", jump, basis_y, precision=HI)
    face = jnp.einsum("sxj,xi->sij", face, basis_x, precision=HI) * face_stiff
    face = jnp.einsum("sij,xi->sxj", face, basis_x, precision=HI)
    face = jnp.einsum("sxj,yj->sxy", face, basis_y, precision=HI)
    weights = 0.5 * (rho + jnp.roll(rho, -1))
    search = weights[:, None, None] * face
    alpha = jnp.sum(jump * search) / (jnp.sum(search * search) + 1e-06)
    return jump, search, alpha


def on_device(
    source, coarse, rho, basis_x, basis_y, basis_z, eigen_x, eigen_y, eigen_z, face_stiff
):
    field = source[0]
    rows, width = field.shape[:2]
    sub_index = lax.axis_index("sub")
    slab_index = lax.axis_index("slab")
    subs = lax.axis_size("sub")
    slabs = lax.axis_size("slab")
    own_rho = lax.dynamic_slice_in_dim(rho, sub_index, 1, 0)[0]
    piece = width // CHUNKS
    lot = piece // slabs
    edge_basis = jnp.stack([basis_z[0], basis_z[width - 1]])

    part = jnp.einsum("xyz,zk->xyk", field + coarse[1, 0], basis_z, precision=MID)
    lines = []
    for c in range(CHUNKS):
        some = jnp.einsum("xyk,yj->xjk", part, basis_y[:, c * piece : (c + 1) * piece], precision=MID)
        lines.append(lax.all_to_all(some, "slab", split_axis=1, concat_axis=0, tiled=True))

    early = jnp.einsum("xyz,zk->xyk", field + coarse[0, 0], basis_z, precision=MID)
    early = jnp.einsum("xyk,yj->jxk", early, basis_y, precision=MID)
    spread_out = lambda column: jnp.broadcast_to(column[:, None], (width, width))
    share = partial_edges(
        early,
        lax.dynamic_slice_in_dim(basis_x, slab_index * rows, rows, 0),
        eigen_y[:, None] + eigen_x[None, :],
        spread_out(eigen_z),
        spread_out(basis_z[0]),
        spread_out(basis_z[width - 1]),
    )
    edges = lax.psum_scatter(share, "slab", scatter_dimension=0, tiled=True) / own_rho
    edges = lax.all_gather(edges, ("sub", "slab"), axis=0, tiled=True)
    edges = edges.reshape(subs, width, 2, width)
    _, search, alpha = face_step(edges, rho, basis_x, basis_y, face_stiff)
    multipliers = alpha * search
    pair = jnp.stack([
        lax.dynamic_index_in_dim(multipliers, (sub_index + subs - 1) % subs, 0, keepdims=False),
        -lax.dynamic_index_in_dim(multipliers, sub_index, 0, keepdims=False),
    ])
    pair = jnp.einsum("pxy,yj->pxj", pair, basis_y, precision=HI)
    pair = jnp.einsum("pxj,xi->pij", pair, basis_x, precision=HI)

    fields = []
    edges = []
    for c in range(CHUNKS):
        start = c * piece + slab_index * lot
        eigen_part = lax.dynamic_slice_in_dim(eigen_y, start, lot, 0)
        pair_part = lax.dynamic_slice_in_dim(pair, start, lot, 2)
        denom = (eigen_x[:, None, None] + eigen_part[None, :, None] + eigen_z[None, None, :]) * own_rho
        hat = jnp.einsum("xjk,xi->ijk", lines[c], basis_x, precision=MID)
        hat = hat + pair_part[0][:, :, None] * edge_basis[0] + pair_part[1][:, :, None] * edge_basis[1]
        modes = hat / denom
        spread = jnp.einsum("ijk,xi->xjk", modes, basis_x, precision=MID)
        fields.append(lax.all_to_all(spread, "slab", split_axis=0, concat_axis=1, tiled=True))
        edges.append(jnp.einsum("ijk,pk->jpi", modes, edge_basis, precision=HI))

    edges = lax.all_gather(jnp.stack(edges), ("sub", "slab"), axis=0, tiled=False)
    edges = edges.reshape(subs, slabs, CHUNKS, lot, 2, width).swapaxes(1, 2).reshape(subs, width, 2, width)
    jump, search, alpha = face_step(edges, rho, basis_x, basis_y, face_stiff)
    multipliers = multipliers + alpha * search

    def own(face):
        face = lax.dynamic_index_in_dim(face, sub_index, 0, keepdims=True)
        return lax.dynamic_slice_in_dim(face, slab_index * rows, rows, 1)

    fields = [jnp.einsum("xjk,zk->xjz", some, basis_z, precision=MID) for some in fields]
    solution = jnp.einsum("xjz,yj->xyz", jnp.concatenate(fields, axis=1), basis_y, precision=MID)
    return (solution[None], own(multipliers), own(jump))


def solution(mesh):
    in_specs = (
        P("sub", "slab", None, None),
        P(None, "sub", "slab", None, None),
        P(),
        P(),
        P(),
        P(),
        P(),
        P(),
        P(),
        P(),
    )
    out_specs = (P("sub", "slab", None, None), P("sub", "slab", None), P("sub", "slab", None))
    return jax.shard_map(
        on_device, mesh=mesh, in_specs=in_specs, out_specs=out_specs, check_vma=False
    )
```

```python
import jax
import jax.numpy as jnp
from jax import lax
from jax.experimental import pallas as pl
from jax.experimental.pallas import tpu as pltpu
from jax.sharding import PartitionSpec as P

ITERS = 2
CHUNKS = 4

HI = lax.Precision.HIGHEST
MID = lax.Precision.HIGH
F32 = jnp.float32
BF16 = jnp.bfloat16


def split(value):
    top = value.astype(BF16)
    return top, (value - top.astype(F32)).astype(BF16)


def edge_kernel(part_ref, basis_ref, pair_ref, eigen_ref, first_ref, last_ref, out_ref):
    top, low = split(basis_ref[...])
    right = jnp.concatenate([top, low, top], axis=0)
    for at in range(part_ref.shape[0]):
        top, low = split(part_ref[at])
        left = jnp.concatenate([top, top, low], axis=0)
        hat = lax.dot_general(left, right, (((0,), (0,)), ((), ())), preferred_element_type=F32)
        modes = hat / (pair_ref[at : at + 1, :] + eigen_ref[...])
        width = basis_ref.shape[1]
        out_ref[at : at + 1, :width] = jnp.sum(modes * first_ref[...], axis=0, keepdims=True)
        out_ref[at : at + 1, width:] = jnp.sum(modes * last_ref[...], axis=0, keepdims=True)


def partial_edges(part, basis_rows, pair, eigen, first, last):
    width, rows, depth = part.shape
    block = 8
    whole = lambda j: (0, 0)
    return pl.pallas_call(
        edge_kernel,
        out_shape=jax.ShapeDtypeStruct((width, 2 * width), F32),
        grid=(width // block,),
        in_specs=[
            pl.BlockSpec((block, rows, depth), lambda j: (j, 0, 0)),
            pl.BlockSpec((rows, width), whole),
            pl.BlockSpec((block, width), lambda j: (j, 0)),
            pl.BlockSpec((depth, width), whole),
            pl.BlockSpec((depth, width), whole),
            pl.BlockSpec((depth, width), whole),
        ],
        out_specs=pl.BlockSpec((block, 2 * width), lambda j: (j, 0)),
        compiler_params=pltpu.CompilerParams(vmem_limit_bytes=24 * 2**20),
        cost_estimate=pl.CostEstimate(
            flops=2 * width * width * depth * 96, bytes_accessed=4 * width * rows * depth, transcendentals=0
        ),
        name="partial_edges",
    )(part, basis_rows, pair, eigen, first, last)


def last_kernel(*refs):
    basis_ref, out_ref = refs[-2:]
    top, low = split(basis_ref[...])
    left = jnp.concatenate([top, top, low], axis=1)
    for at in range(out_ref.shape[0]):
        top, low = split(jnp.concatenate([ref[at] for ref in refs[:-2]], axis=0))
        right = jnp.concatenate([top, low, top], axis=0)
        out_ref[at] = jnp.dot(left, right, preferred_element_type=F32)


def last_product(fields, basis_y):
    rows, piece, depth = fields[0].shape
    width = basis_y.shape[0]
    block = 4
    return pl.pallas_call(
        last_kernel,
        out_shape=jax.ShapeDtypeStruct((rows, width, depth), F32),
        grid=(rows // block,),
        in_specs=[pl.BlockSpec((block, piece, depth), lambda x: (x, 0, 0))] * len(fields)
        + [pl.BlockSpec((width, width), lambda x: (0, 0))],
        out_specs=pl.BlockSpec((block, width, depth), lambda x: (x, 0, 0)),
        compiler_params=pltpu.CompilerParams(vmem_limit_bytes=24 * 2**20),
        name="last_product",
    )(*fields, basis_y)


def from_behind(block, axis, distance):
    count = lax.axis_size(axis)
    return lax.ppermute(block, axis, [((i - distance) % count, i) for i in range(count)])


def exchange(blocks, extra, before):
    size = blocks.shape[1]
    if extra is not None:
        blocks = jnp.concatenate([blocks, extra], axis=1)
    if before:
        blocks, _ = lax.optimization_barrier((blocks, before[-1]))
    got = lax.all_to_all(blocks, "slab", split_axis=0, concat_axis=0, tiled=True)
    before.append(got)
    return got[:, :size], got[:, size:]


def face_step(apart, weight, basis_x, basis_y, face_stiff):
    subs = lax.axis_size("sub")
    jump = jnp.einsum("ji,yj->yi", apart, basis_y, precision=HI)
    jump = jnp.einsum("yi,xi->xy", jump, basis_x, precision=HI)
    face = jnp.einsum("xy,yj->xj", jump, basis_y, precision=HI)
    face = jnp.einsum("xj,xi->ij", face, basis_x, precision=HI) * face_stiff
    face = jnp.einsum("ij,xi->xj", face, basis_x, precision=HI)
    face = jnp.einsum("xj,yj->xy", face, basis_y, precision=HI)
    search = weight * face
    sums = jnp.stack([jnp.sum(jump * search), jnp.sum(search * search)])
    sums = jnp.broadcast_to(sums[:, None], (2, 128))
    total = sums
    for distance in range(1, subs):
        total = total + from_behind(sums, "sub", distance)
    return jump, search, total[0, 0] / (total[1, 0] + 1e-06)


def on_device(
    source, coarse, rho, basis_x, basis_y, basis_z, eigen_x, eigen_y, eigen_z, face_stiff
):
    field = source[0]
    rows, width = field.shape[:2]
    sub_index = lax.axis_index("sub")
    slab_index = lax.axis_index("slab")
    subs = lax.axis_size("sub")
    slabs = lax.axis_size("slab")
    own_rho = lax.dynamic_slice_in_dim(rho, sub_index, 1, 0)[0]
    next_rho = lax.dynamic_slice_in_dim(rho, (sub_index + 1) % subs, 1, 0)[0]
    weight = 0.5 * (own_rho + next_rho)
    piece = width // CHUNKS
    lot = piece // slabs
    edge_basis = jnp.stack([basis_z[0], basis_z[width - 1]])
    before = []

    part = jnp.einsum("xyz,zk->xyk", field + coarse[1, 0], basis_z, precision=MID)

    def outward(c, extra=None):
        some = jnp.einsum("xyk,yj->xjk", part, basis_y[:, c * piece : (c + 1) * piece], precision=MID)
        some = some.reshape(rows, slabs, lot, width).swapaxes(0, 1)
        some, extra = exchange(some, extra, before)
        return some.reshape(width, lot, width), extra

    lines = [outward(0)[0]]

    early = jnp.einsum("xyz,zk->xyk", field + coarse[0, 0], basis_z, precision=MID)
    early = jnp.einsum("xyk,yj->jxk", early, basis_y, precision=MID)
    spread_out = lambda column: jnp.broadcast_to(column[:, None], (width, width))
    share = partial_edges(
        early,
        lax.dynamic_slice_in_dim(basis_x, slab_index * rows, rows, 0),
        eigen_y[:, None] + eigen_x[None, :],
        spread_out(eigen_z),
        spread_out(basis_z[0]),
        spread_out(basis_z[width - 1]),
    )
    some, extra = outward(1, share.reshape(slabs, 2 * CHUNKS, lot, width))
    lines.append(some)
    edges = jnp.sum(extra, axis=0).reshape(width // slabs, 2 * width) / own_rho
    apart = edges[:, width:] - from_behind(edges[:, :width], "sub", -1)
    apart = jnp.broadcast_to(apart.reshape(1, CHUNKS, lot, width), (slabs, CHUNKS, lot, width))
    some, extra = outward(2, apart)
    lines.append(some)
    lines.append(outward(3)[0])
    _, search, alpha = face_step(extra.reshape(width, width), weight, basis_x, basis_y, face_stiff)
    multipliers = alpha * search
    pair = jnp.stack([alpha * from_behind(search, "sub", 1), -multipliers])
    pair = jnp.einsum("pxy,yj->pxj", pair, basis_y, precision=HI)
    pair = jnp.einsum("pxj,xi->pij", pair, basis_x, precision=HI)

    def modal(c):
        start = c * piece + slab_index * lot
        eigen_part = lax.dynamic_slice_in_dim(eigen_y, start, lot, 0)
        pair_part = lax.dynamic_slice_in_dim(pair, start, lot, 2)
        denom = (eigen_x[:, None, None] + eigen_part[None, :, None] + eigen_z[None, None, :]) * own_rho
        hat = jnp.einsum("xjk,xi->ijk", lines[c], basis_x, precision=MID)
        hat = hat + pair_part[0][:, :, None] * edge_basis[0] + pair_part[1][:, :, None] * edge_basis[1]
        modes = hat / denom
        spread = jnp.einsum("ijk,xi->xjk", modes, basis_x, precision=MID)
        edges = jnp.einsum("ijk,pk->pji", modes, edge_basis, precision=HI)
        return spread.reshape(slabs, rows, lot, width), edges

    def inward(spread, extra=None):
        some, extra = exchange(spread, extra, before)
        some = jnp.einsum("dxjk,zk->xdjz", some, basis_z, precision=MID)
        return some.reshape(rows, piece, width), extra

    spreads, edges = zip(*[modal(c) for c in range(CHUNKS)])
    edges = jnp.stack(edges, axis=1)
    apart = edges[1] - from_behind(edges[0], "sub", -1)
    apart = jnp.broadcast_to(apart[None], (slabs, CHUNKS, lot, width))
    fields = [inward(spreads[0])[0], inward(spreads[1])[0]]
    some, extra = inward(spreads[2], apart)
    fields.append(some)
    extra = extra.swapaxes(0, 1).reshape(width, width)
    jump, search, alpha = face_step(extra, weight, basis_x, basis_y, face_stiff)
    multipliers = multipliers + alpha * search
    own = lambda face: lax.dynamic_slice_in_dim(face, slab_index * rows, rows, 0)
    fields.append(inward(spreads[3])[0])
    solution = last_product(fields, basis_y)
    return (solution[None], own(multipliers)[None], own(jump)[None])


def solution(mesh):
    in_specs = (
        P("sub", "slab", None, None),
        P(None, "sub", "slab", None, None),
        P(),
        P(),
        P(),
        P(),
        P(),
        P(),
        P(),
        P(),
    )
    out_specs = (P("sub", "slab", None, None), P("sub", "slab", None), P("sub", "slab", None))
    return jax.shard_map(
        on_device, mesh=mesh, in_specs=in_specs, out_specs=out_specs, check_vma=False
    )
```

```python
import jax
import jax.numpy as jnp
from jax import lax
from jax.experimental.layout import Layout, with_layout_constraint
from jax.experimental import pallas as pl
from jax.experimental.pallas import tpu as pltpu
from jax.sharding import PartitionSpec as P

ITERS = 2
CHUNKS = 4

HI = lax.Precision.HIGHEST
MID = lax.Precision.HIGH
F32 = jnp.float32
BF16 = jnp.bfloat16


def split(value):
    top = value.astype(BF16)
    return top, (value - top.astype(F32)).astype(BF16)


def edge_kernel(part_ref, basis_ref, pair_ref, eigen_ref, first_ref, last_ref, out_ref):
    top, low = split(basis_ref[...])
    right = jnp.concatenate([top, low, top], axis=0)
    for at in range(part_ref.shape[1]):
        top, low = split(part_ref[:, at, :])
        left = jnp.concatenate([top, top, low], axis=0)
        hat = lax.dot_general(left, right, (((0,), (0,)), ((), ())), preferred_element_type=F32)
        modes = hat / (pair_ref[at : at + 1, :] + eigen_ref[...])
        width = basis_ref.shape[1]
        out_ref[at : at + 1, :width] = jnp.sum(modes * first_ref[...], axis=0, keepdims=True)
        out_ref[at : at + 1, width:] = jnp.sum(modes * last_ref[...], axis=0, keepdims=True)


def partial_edges(part, basis_rows, pair, eigen, first, last):
    rows, width, depth = part.shape
    block = 8
    whole = lambda j: (0, 0)
    return pl.pallas_call(
        edge_kernel,
        out_shape=jax.ShapeDtypeStruct((width, 2 * width), F32),
        grid=(width // block,),
        in_specs=[
            pl.BlockSpec((rows, block, depth), lambda j: (0, j, 0)),
            pl.BlockSpec((rows, width), whole),
            pl.BlockSpec((block, width), lambda j: (j, 0)),
            pl.BlockSpec((depth, width), whole),
            pl.BlockSpec((depth, width), whole),
            pl.BlockSpec((depth, width), whole),
        ],
        out_specs=pl.BlockSpec((block, 2 * width), lambda j: (j, 0)),
        compiler_params=pltpu.CompilerParams(vmem_limit_bytes=24 * 2**20),
        cost_estimate=pl.CostEstimate(
            flops=2 * width * width * depth * 96, bytes_accessed=4 * width * rows * depth, transcendentals=0
        ),
        name="partial_edges",
    )(part, basis_rows, pair, eigen, first, last)


def last_kernel(*refs):
    basis_ref, out_ref = refs[-2:]
    top, low = split(basis_ref[...])
    left = jnp.concatenate([top, top, low], axis=1)
    for at in range(out_ref.shape[0]):
        top, low = split(jnp.concatenate([ref[at] for ref in refs[:-2]], axis=0))
        right = jnp.concatenate([top, low, top], axis=0)
        out_ref[at] = jnp.dot(left, right, preferred_element_type=F32)


def last_product(fields, basis_y):
    rows, piece, depth = fields[0].shape
    width = basis_y.shape[0]
    block = 4
    return pl.pallas_call(
        last_kernel,
        out_shape=jax.ShapeDtypeStruct((rows, width, depth), F32),
        grid=(rows // block,),
        in_specs=[pl.BlockSpec((block, piece, depth), lambda x: (x, 0, 0))] * len(fields)
        + [pl.BlockSpec((width, width), lambda x: (0, 0))],
        out_specs=pl.BlockSpec((block, width, depth), lambda x: (x, 0, 0)),
        compiler_params=pltpu.CompilerParams(vmem_limit_bytes=24 * 2**20),
        name="last_product",
    )(*fields, basis_y)


def from_behind(block, axis, distance):
    count = lax.axis_size(axis)
    return lax.ppermute(block, axis, [((i - distance) % count, i) for i in range(count)])


def exchange(blocks, extra, before):
    size = blocks.shape[1]
    if extra is not None:
        blocks = jnp.concatenate([blocks, extra], axis=1)
    if before:
        blocks = with_layout_constraint(blocks, Layout(major_to_minor=(0, 1, 2, 3)))
        blocks, _ = lax.optimization_barrier((blocks, before[-1]))
    got = lax.all_to_all(blocks, "slab", split_axis=0, concat_axis=0, tiled=True)
    before.append(got)
    return got[:, :size], got[:, size:]


def face_step(apart, weight, basis_x, basis_y, face_stiff):
    subs = lax.axis_size("sub")
    jump = jnp.einsum("ji,yj->yi", apart, basis_y, precision=HI)
    jump = jnp.einsum("yi,xi->xy", jump, basis_x, precision=HI)
    face = jnp.einsum("xy,yj->xj", jump, basis_y, precision=HI)
    face = jnp.einsum("xj,xi->ij", face, basis_x, precision=HI) * face_stiff
    face = jnp.einsum("ij,xi->xj", face, basis_x, precision=HI)
    face = jnp.einsum("xj,yj->xy", face, basis_y, precision=HI)
    search = weight * face
    sums = jnp.stack([jnp.sum(jump * search), jnp.sum(search * search)])
    sums = jnp.broadcast_to(sums[:, None], (2, 128))
    total = sums
    for distance in range(1, subs):
        total = total + from_behind(sums, "sub", distance)
    return jump, search, total[0, 0] / (total[1, 0] + 1e-06)


def on_device(
    source, coarse, rho, basis_x, basis_y, basis_z, eigen_x, eigen_y, eigen_z, face_stiff
):
    field = source[0]
    rows, width = field.shape[:2]
    sub_index = lax.axis_index("sub")
    slab_index = lax.axis_index("slab")
    subs = lax.axis_size("sub")
    slabs = lax.axis_size("slab")
    own_rho = lax.dynamic_slice_in_dim(rho, sub_index, 1, 0)[0]
    next_rho = lax.dynamic_slice_in_dim(rho, (sub_index + 1) % subs, 1, 0)[0]
    weight = 0.5 * (own_rho + next_rho)
    piece = width // CHUNKS
    lot = piece // slabs
    edge_basis = jnp.stack([basis_z[0], basis_z[width - 1]])
    before = []

    part = jnp.einsum("xyz,zk->xyk", field + coarse[1, 0], basis_z, precision=MID)

    def outward(c, extra=None):
        some = jnp.einsum("xyk,yj->xjk", part, basis_y[:, c * piece : (c + 1) * piece], precision=MID)
        some = some.reshape(rows, slabs, lot, width).swapaxes(0, 1)
        some, extra = exchange(some, extra, before)
        return some.reshape(width, lot, width), extra

    lines = [outward(0)[0]]

    early = jnp.einsum("xyz,zk->xyk", field + coarse[0, 0], basis_z, precision=MID)
    early = jnp.einsum("xyk,yj->xjk", early, basis_y, precision=MID)
    spread_out = lambda column: jnp.broadcast_to(column[:, None], (width, width))
    share = partial_edges(
        early,
        lax.dynamic_slice_in_dim(basis_x, slab_index * rows, rows, 0),
        eigen_y[:, None] + eigen_x[None, :],
        spread_out(eigen_z),
        spread_out(basis_z[0]),
        spread_out(basis_z[width - 1]),
    )
    some, extra = outward(1, share.reshape(slabs, 2 * CHUNKS, lot, width))
    lines.append(some)
    edges = jnp.sum(extra, axis=0).reshape(width // slabs, 2 * width) / own_rho
    apart = edges[:, width:] - from_behind(edges[:, :width], "sub", -1)
    apart = jnp.broadcast_to(apart.reshape(1, CHUNKS, lot, width), (slabs, CHUNKS, lot, width))
    some, extra = outward(2, apart)
    lines.append(some)
    lines.append(outward(3)[0])
    _, search, alpha = face_step(extra.reshape(width, width), weight, basis_x, basis_y, face_stiff)
    multipliers = alpha * search
    pair = jnp.stack([alpha * from_behind(search, "sub", 1), -multipliers])
    pair = jnp.einsum("pxy,yj->pxj", pair, basis_y, precision=HI)
    pair = jnp.einsum("pxj,xi->pij", pair, basis_x, precision=HI)

    def modal(c):
        start = c * piece + slab_index * lot
        eigen_part = lax.dynamic_slice_in_dim(eigen_y, start, lot, 0)
        pair_part = lax.dynamic_slice_in_dim(pair, start, lot, 2)
        denom = (eigen_x[:, None, None] + eigen_part[None, :, None] + eigen_z[None, None, :]) * own_rho
        hat = jnp.einsum("xjk,xi->ijk", lines[c], basis_x, precision=MID)
        hat = hat + pair_part[0][:, :, None] * edge_basis[0] + pair_part[1][:, :, None] * edge_basis[1]
        modes = hat / denom
        spread = jnp.einsum("ijk,xi->xjk", modes, basis_x, precision=MID)
        edges = jnp.einsum("ijk,pk->pji", modes, edge_basis, precision=HI)
        return spread.reshape(slabs, rows, lot, width), edges

    def inward(spread, extra=None):
        some, extra = exchange(spread, extra, before)
        some = jnp.einsum("dxjk,zk->xdjz", some, basis_z, precision=MID)
        return some.reshape(rows, piece, width), extra

    spreads, edges = zip(*[modal(c) for c in range(CHUNKS)])
    edges = jnp.stack(edges, axis=1)
    apart = edges[1] - from_behind(edges[0], "sub", -1)
    apart = jnp.broadcast_to(apart[None], (slabs, CHUNKS, lot, width))
    fields = [inward(spreads[0])[0], inward(spreads[1])[0]]
    some, extra = inward(spreads[2], apart)
    fields.append(some)
    extra = extra.swapaxes(0, 1).reshape(width, width)
    jump, search, alpha = face_step(extra, weight, basis_x, basis_y, face_stiff)
    multipliers = multipliers + alpha * search
    own = lambda face: lax.dynamic_slice_in_dim(face, slab_index * rows, rows, 0)
    fields.append(inward(spreads[3])[0])
    solution = last_product(fields, basis_y)
    return (solution[None], own(multipliers)[None], own(jump)[None])


def solution(mesh):
    in_specs = (
        P("sub", "slab", None, None),
        P(None, "sub", "slab", None, None),
        P(),
        P(),
        P(),
        P(),
        P(),
        P(),
        P(),
        P(),
    )
    out_specs = (P("sub", "slab", None, None), P("sub", "slab", None), P("sub", "slab", None))
    return jax.shard_map(
        on_device, mesh=mesh, in_specs=in_specs, out_specs=out_specs, check_vma=False
    )
```
